256 devices in a mesh: seq: 64 (over x, z_hi, y, core), head: 4 (over z_lo).
Axes of the slice: x: 4, y: 4, z: 8 (z_hi: 2, z_lo: 4; z = z_hi * 4 + z_lo), core: 2. Of those that a mesh axis runs over, the one named last changes fastest.
Arguments:
- video: bfloat16 [16384, 3072], P('seq'), may hold values from -6 to 6
- cotangent: bfloat16 [16384, 3072], P('seq'), may hold values from -48 to 48
- text_embed: bfloat16 [256, 4096], P(None, 'seq'), may hold values from -700 to 700
- text_gain: float32 [4096], P('seq'), may hold values from 0.25 to 1.75
- w_query: bfloat16 [3072, 3072], P('seq', 'head'), may hold values from -0.109375 to 0.109375
- w_key: bfloat16 [4096, 3072], P('seq', 'head'), may hold values from -0.09375 to 0.09375
- w_value: bfloat16 [4096, 3072], P('seq', 'head'), may hold values from -0.09375 to 0.09375
- w_out: bfloat16 [3072, 3072], P('head', 'seq'), may hold values from -0.109375 to 0.109375
Outputs:
- grad_video: bfloat16 [16384, 3072], P('seq', 'head')
- grad_text: float32 [256, 4096], P(None, 'seq')
The draws below stay inside these ranges and needn't reach their ends.
All inputs are finite; a program needn't handle non-finite values.
Results may differ from the reference program's by a relative error of at most 0.012.
Values may be sent and summed in bfloat16 or wider, within the bound.
No kernel may reach another device: no remote copies, remote signals or barrier semaphores. Data moves between devices by JAX's collectives and lax.ppermute only.
A program may use at most 64 MiB of HBM per device.

```python
import jax
import jax.numpy as jnp
from jax import lax

D = 3072
HEADS = 24
HEAD_DIM = 128
TEXT_LEN = 256
TEXT_DIM = 4096
TOKENS = 16384


def draw_text_embed(key, part):
    key_rows, key_cols, key_main = jax.random.split(key, 3)
    row_scale = 10.0 ** jax.random.uniform(key_rows, (TEXT_LEN, 1), jnp.float32)
    column = jnp.arange(TEXT_DIM, dtype=jnp.float32)
    trend = jnp.sqrt(1.0 + 2.0 * column / max(TEXT_DIM - 1, 1))
    col_scale = 10.0 ** jax.random.uniform(key_cols, (1, TEXT_DIM), jnp.float32) * trend[None, :]
    entries = jnp.clip(jax.random.normal(key_main, (TEXT_LEN, TEXT_DIM), jnp.float32), -4.0, 4.0)
    return (entries * row_scale * col_scale).astype(jnp.bfloat16)


def level_of(stream_key, extent, shards, smallest, high):
    level, own = 1.0, jax.random.fold_in(stream_key, 6)
    for position, blocks in shards:
        steps = jnp.exp(jax.random.uniform(jax.random.fold_in(own, position), (blocks,), jnp.float32, smallest / len(shards), high / len(shards)))
        level = level * jnp.repeat(steps, extent[position] // blocks).reshape([-1 if axis == position else 1 for axis in range(len(extent))])
    return level


def gaussian(rng, extent, width, most, cuts=(), kind=jnp.bfloat16):
    drawn = jax.random.normal(rng, extent, jnp.float32) * width
    if len(cuts) > 0:
        drawn = level_of(rng, extent, cuts, -0.22, 0.18) * drawn
    return jnp.clip(drawn, min=-most, max=most).astype(kind)


def setup_inputs(seed: int = 0) -> dict:
    arg_keys = jax.random.split(jax.random.key(seed), 9)
    return {
        "video": gaussian(arg_keys[0], (TOKENS, D), 1.0, 6.0, ((0, 64),)),
        "cotangent": gaussian(arg_keys[1], (TOKENS, D), 8.0, 48.0, ((0, 64),)),
        "text_embed": draw_text_embed(jax.random.fold_in(arg_keys[8], 71), 0),
        "text_gain": jnp.clip(1.0 + 0.15 * jax.random.normal(arg_keys[3], (TEXT_DIM,), jnp.float32), 0.25, 1.75),
        "w_query": gaussian(arg_keys[4], (D, HEADS * HEAD_DIM), D ** -0.5, 0.109375, ((0, 64), (1, 4))),
        "w_key": gaussian(arg_keys[5], (TEXT_DIM, HEADS * HEAD_DIM), TEXT_DIM ** -0.5, 0.09375, ((0, 64), (1, 4))),
        "w_value": gaussian(arg_keys[6], (TEXT_DIM, HEADS * HEAD_DIM), TEXT_DIM ** -0.5, 0.09375, ((0, 64), (1, 4))),
        "w_out": gaussian(arg_keys[7], (HEADS * HEAD_DIM, D), (HEADS * HEAD_DIM) ** -0.5, 0.109375, ((0, 4), (1, 64))),
    }


epsilon = 1e-06

def one_head(operands):
    query_head, key_head, value_head, grad_head = operands
    score_scale = HEAD_DIM ** (-0.5)
    scores = jnp.dot(query_head, key_head.T, preferred_element_type=jnp.float32) * score_scale
    raised = jnp.exp(scores)
    softmax_out = raised / lax.optimization_barrier(jnp.sum(raised, axis=1, keepdims=True))
    grad_probs = jnp.dot(grad_head, value_head.T, preferred_element_type=jnp.float32)
    row_delta = lax.optimization_barrier(jnp.sum(grad_probs * softmax_out, axis=1, keepdims=True))
    grad_scores = (softmax_out * (grad_probs - row_delta) * score_scale).astype(jnp.bfloat16)
    grad_query = jnp.dot(grad_scores, key_head, preferred_element_type=jnp.float32).astype(jnp.bfloat16)
    grad_key = jnp.dot(grad_scores.T, query_head, preferred_element_type=jnp.float32)
    grad_value = jnp.dot(softmax_out.astype(jnp.bfloat16).T, grad_head, preferred_element_type=jnp.float32)
    return (grad_query, grad_key, grad_value)

def by_heads(matrix, count):
    return matrix.reshape(count, HEADS, HEAD_DIM).transpose(1, 0, 2)

def from_heads(stacked, count):
    return stacked.transpose(1, 0, 2).reshape(count, HEADS * HEAD_DIM)

def reference(video, cotangent, text_embed, text_gain, w_query, w_key, w_value, w_out):
    contract = (((1,), (1,)), ((), ()))
    text_wide = text_embed.astype(jnp.float32)
    inverse_rms = lax.rsqrt(lax.optimization_barrier(jnp.sum(text_wide * text_wide, axis=1, keepdims=True)) / TEXT_DIM + epsilon)
    scaled_text = (text_wide * text_gain).astype(jnp.bfloat16)
    keys = (inverse_rms * jnp.dot(scaled_text, w_key, preferred_element_type=jnp.float32)).astype(jnp.bfloat16)
    text_values = (inverse_rms * jnp.dot(scaled_text, w_value, preferred_element_type=jnp.float32)).astype(jnp.bfloat16)
    query = jnp.dot(video, w_query, preferred_element_type=jnp.float32).astype(jnp.bfloat16)
    grad_out = lax.dot_general(cotangent, w_out, contract, preferred_element_type=jnp.float32).astype(jnp.bfloat16)
    grad_query, grad_keys, grad_values = lax.map(one_head, (by_heads(query, TOKENS), by_heads(keys, TEXT_LEN), by_heads(text_values, TEXT_LEN), by_heads(grad_out, TOKENS)))
    grad_query = from_heads(grad_query, TOKENS)
    grad_video = lax.dot_general(grad_query, w_query, contract, preferred_element_type=jnp.float32).astype(jnp.bfloat16)
    keys_low = from_heads(grad_keys, TEXT_LEN).astype(jnp.bfloat16)
    values_low = from_heads(grad_values, TEXT_LEN).astype(jnp.bfloat16)
    grad_normed = lax.dot_general(keys_low, w_key, contract, preferred_element_type=jnp.float32) + lax.dot_general(values_low, w_value, contract, preferred_element_type=jnp.float32)
    normed = text_wide * inverse_rms
    row_stat = lax.optimization_barrier(jnp.sum(grad_normed * text_gain * normed, axis=1, keepdims=True))
    grad_text = inverse_rms * (grad_normed * text_gain - normed * (row_stat / TEXT_DIM))
    return (grad_video, grad_text)
```

```python
import jax
import jax.numpy as jnp
from jax import lax
from jax.experimental import pallas as pl
from jax.experimental.pallas import tpu as pltpu
from jax.sharding import Mesh
from jax.sharding import PartitionSpec as P

HEAD_DIM = 128
TEXT_DIM = 4096
EPSILON = 1e-06
SCALE = HEAD_DIM ** (-0.5)


BF = jnp.bfloat16
F32 = jnp.float32
SIZES = {"x": 4, "zhi": 2, "y": 4, "c": 2, "zlo": 4}
NT = (((1,), (1,)), ((), ()))
TN = (((0,), (0,)), ((), ()))


def shift(a, axis, by):
    n = SIZES[axis]
    return lax.ppermute(a, axis, [(i, (i + by) % n) for i in range(n)])


def gather(a, axis):
    return [a, shift(a, axis, -1), shift(a, axis, 2), shift(a, axis, 1)]


def scatter_sum(pieces, axis):
    n1 = shift(pieces[1].astype(pieces[-1].dtype), axis, 1)
    n2 = shift(pieces[2].astype(pieces[-1].dtype), axis, 2)
    n3 = shift(pieces[3], axis, -1)
    return (pieces[0].astype(F32) + n2.astype(F32)) + (n1.astype(F32) + n3.astype(F32))


def split_pair(v):
    hi = v.astype(BF)
    lo = (v - hi.astype(F32)).astype(BF)
    return hi, lo


def place(idx, dst_ref, parts, x_major):
    x, zhi, y = idx[0], idx[1], idx[2]
    for k, part in enumerate(parts):
        for j in range(4):
            for kz in range(2):
                kx, ky = (j, k) if x_major else (k, j)
                block = ((x + kx) & 3) * 8 + ((zhi + kz) & 1) * 4 + ((y + ky) & 3)
                row = pl.multiple_of(block * 96, 96)
                dst_ref[pl.ds(row, 96), :] = part[pl.ds((j * 2 + kz) * 96, 96), :]


def attention_kernel(idx, v0, v1, c0, c1, q0, q1, q2, q3, o0, o1, o2, o3, kv,
                     gq0, gq1, gown, g1, g2, g3, wq, wo, acc):
    place(idx, wq, (q0, q1, q2, q3), True)
    place(idx, wo, (o0, o1, o2, o3), False)
    acc[...] = jnp.zeros_like(acc)
    rows = 128
    for v, c, gq in ((v0, c0, gq0), (v1, c1, gq1)):

        def tile(t, carry, v=v, c=c, gq=gq):
            at = pl.ds(pl.multiple_of(t * rows, rows), rows)
            query = jnp.dot(v[at, :], wq[...], preferred_element_type=F32).astype(BF)
            grad = jnp.dot(c[at, :], wo[...], preferred_element_type=F32).astype(BF)
            for h in range(3):
                lanes = slice(h * 128, h * 128 + 128)
                vlanes = slice(384 + h * 128, 512 + h * 128)
                qh, gh = query[:, lanes], grad[:, lanes]
                kh, vh = kv[:, lanes], kv[:, vlanes]
                raised = jnp.exp(lax.dot_general(qh, kh, NT, preferred_element_type=F32) * SCALE)
                probs = raised * (1.0 / jnp.sum(raised, axis=1, keepdims=True))
                gp = lax.dot_general(gh, vh, NT, preferred_element_type=F32)
                delta = jnp.sum(gp * probs, axis=1, keepdims=True)
                gs = (probs * (gp - delta) * SCALE).astype(BF)
                gq[at, lanes] = jnp.dot(gs, kh, preferred_element_type=F32).astype(BF)
                acc[:, lanes] += lax.dot_general(gs, qh, TN, preferred_element_type=F32)
                acc[:, vlanes] += lax.dot_general(
                    probs.astype(BF), gh, TN, preferred_element_type=F32
                )
            return carry

        lax.fori_loop(0, v.shape[0] // rows, tile, 0)
    gown[...] = acc[0:64, :]
    g1[...] = acc[64:128, :].astype(BF)
    g2[...] = acc[128:192, :].astype(BF)
    g3[...] = acc[192:256, :].astype(BF)


def video_kernel(idx, gq0, gq1, wq, p0, p1, p2, p3, r0, r1, r2, r3, wp):
    place(idx, wp, (p0, p1, p2, p3), True)
    zlo = idx[3]
    for k, out in enumerate((r0, r1, r2, r3)):
        at = pl.ds(pl.multiple_of(((zlo + k) & 3) * 768, 768), 768)
        out[...] = (
            lax.dot_general(gq0[...], wq[at, :], NT, preferred_element_type=F32)
            + lax.dot_general(gq1[...], wp[at, :], NT, preferred_element_type=F32)
        ).astype(BF)


VMEM = pl.BlockSpec(memory_space=pltpu.VMEM)
SMEM = pl.BlockSpec(memory_space=pltpu.SMEM)
PARAMS = pltpu.CompilerParams(vmem_limit_bytes=56 * 1024 * 1024)


def attention(idx, *args):
    shapes = [((256, 384), BF)] * 2 + [((64, 768), F32)] + [((64, 768), BF)] * 3 + [((3072, 384), BF)]
    return pl.pallas_call(
        attention_kernel,
        out_shape=tuple(jax.ShapeDtypeStruct(s, d) for s, d in shapes),
        in_specs=[SMEM] + [VMEM] * len(args),
        out_specs=tuple([VMEM] * len(shapes)),
        scratch_shapes=[pltpu.VMEM((3072, 384), BF), pltpu.VMEM((256, 768), F32)],
        compiler_params=PARAMS,
        cost_estimate=pl.CostEstimate(flops=3 * 10**9, bytes_accessed=20 * 10**6, transcendentals=400000),
    )(idx, *args)


def video_terms(idx, *args):
    return pl.pallas_call(
        video_kernel,
        out_shape=tuple(jax.ShapeDtypeStruct((256, 768), BF) for _ in range(4)),
        in_specs=[SMEM] + [VMEM] * len(args),
        out_specs=tuple([VMEM] * 4),
        scratch_shapes=[pltpu.VMEM((3072, 384), BF)],
        compiler_params=PARAMS,
        cost_estimate=pl.CostEstimate(flops=12 * 10**8, bytes_accessed=7 * 10**6, transcendentals=0),
    )(idx, *args)


def body(video, cotangent, text_embed, text_gain, w_query, w_key, w_value, w_out):
    x, zhi, y = lax.axis_index("x"), lax.axis_index("zhi"), lax.axis_index("y")
    zlo, core = lax.axis_index("zlo"), lax.axis_index("c")
    idx = jnp.stack([x, zhi, y, zlo, core]).astype(jnp.int32)
    first = core == 0

    packed = jnp.concatenate([w_query, w_out.T, w_key, w_value], axis=0)
    left, right = packed[:, :384], packed[:, 384:]
    mine = jnp.where(first, left, right)
    other = shift(jnp.where(first, right, left), "c", 1)
    wq_pair = jnp.where(first, jnp.concatenate([mine[0:48], other[0:48]]), jnp.concatenate([other[0:48], mine[0:48]]))
    wo_pair = jnp.where(first, jnp.concatenate([mine[48:96], other[48:96]]), jnp.concatenate([other[48:96], mine[48:96]]))
    shard = jnp.stack([wq_pair, wo_pair])
    shard_z = shift(shard, "zhi", 1)
    wq_parts = gather(jnp.concatenate([shard[0], shard_z[0]]), "x")
    wo_parts = gather(jnp.concatenate([shard[1], shard_z[1]]), "y")
    wq_parts = gather(jnp.concatenate(wq_parts), "y")
    wo_parts = gather(jnp.concatenate(wo_parts), "x")
    wp_parts = [shift(p, "c", 1) for p in wq_parts]

    k = jnp.arange(256)
    rows = ((k // 64 + x) % 4) * 64 + ((k // 16 + y) % 4) * 16 + ((k // 8 + zhi) % 2) * 8 + k % 8
    order = (rows[:, None] == k[None, :]).astype(BF)
    text_wide = text_embed.astype(F32)
    scaled = (text_wide * text_gain).astype(BF)
    sq_hi, sq_lo = split_pair(jnp.sum(text_wide * text_wide, axis=1, keepdims=True))
    text_pack = jnp.concatenate([scaled, sq_hi, sq_lo, jnp.zeros((256, 62), BF)], axis=1)
    text_pack = jnp.dot(order, text_pack, preferred_element_type=F32).astype(BF)
    text_other = shift(text_pack, "c", 1)

    def project(pack, w):
        p = jnp.concatenate([w[96:160], w[160:224]], axis=1)
        return jnp.dot(pack[:, :64], p, preferred_element_type=F32)

    kv_part = project(text_pack, mine) + project(text_other, other)
    sq_part = text_pack[:, 64:66].astype(F32) + text_other[:, 64:66].astype(F32)
    sh, sl = split_pair(jnp.sum(sq_part, axis=1, keepdims=True))
    kv_part = jnp.concatenate([kv_part, sh.astype(F32), sl.astype(F32), jnp.zeros((256, 126), F32)], axis=1)
    low = kv_part.astype(BF)
    part = scatter_sum([kv_part[0:64]] + [low[64 * i : 64 * i + 64] for i in (1, 2, 3)], "x")
    part = scatter_sum([part[16 * i : 16 * i + 16] for i in range(4)], "y")
    other_half = shift(jnp.concatenate([part[8:16], part[0:8]]), "zhi", 1)
    part = part + other_half
    inverse = lax.rsqrt((part[:, 768:769] + part[:, 769:770]) / TEXT_DIM + EPSILON)
    kv_wide = part[:, :768] * inverse
    inv_hi, inv_lo = split_pair(inverse)
    inv_lo2 = ((inverse - inv_hi.astype(F32)) - inv_lo.astype(F32)).astype(BF)
    kv = jnp.concatenate([kv_wide.astype(BF), inv_hi, inv_lo, inv_lo2, jnp.zeros((16, 125), BF)], axis=1)
    kv = jnp.concatenate(gather(jnp.concatenate(gather(kv, "y")), "x"))
    inv_abs = lax.dot_general(order, kv[:, 768:896], TN, preferred_element_type=F32)
    inverse_rms = inv_abs[:, 0:1] + (inv_abs[:, 1:2] + inv_abs[:, 2:3])

    video_o, cot_o = shift(video, "c", 1), shift(cotangent, "c", 1)
    gq_own, gq_send, g0, g1, g2, g3, wq_full = attention(
        idx, video, video_o, cotangent, cot_o, *wq_parts, *wo_parts, kv
    )
    gq_recv = shift(gq_send, "c", 1)
    terms = video_terms(idx, gq_own, gq_recv, wq_full, *wp_parts)
    r1, r2, r3 = shift(terms[1], "zlo", 1), shift(terms[2], "zlo", 2), shift(terms[3], "zlo", 3)
    grad_video = (
        (terms[0].astype(F32) + r1.astype(F32)) + (r2.astype(F32) + r3.astype(F32))
    ).astype(BF)

    part = scatter_sum([g0, g1, g2, g3], "x")
    part = scatter_sum([part[16 * i : 16 * i + 16] for i in range(4)], "y")
    other_half = shift(jnp.concatenate([part[8:16], part[0:8]]), "zhi", 1)
    low = (part + other_half).astype(BF)
    st_hi, st_lo = split_pair(jnp.sum(low.astype(F32) * kv_wide, axis=1, keepdims=True))
    grads = jnp.concatenate([low, st_hi, st_lo, jnp.zeros((16, 126), BF)], axis=1)
    grads = jnp.concatenate(gather(jnp.concatenate(gather(grads, "y")), "x"))
    grads = lax.dot_general(order, grads, TN, preferred_element_type=F32).astype(BF)

    def back(w):
        return lax.dot_general(grads[:, :384], w[96:160], NT, preferred_element_type=F32) + lax.dot_general(
            grads[:, 384:768], w[160:224], NT, preferred_element_type=F32
        )

    stat = grads[:, 768:770]
    tail = jnp.zeros((256, 62), BF)
    partner = shift(jnp.concatenate([back(other).astype(BF), stat, tail], axis=1), "c", 1)
    normed_part = back(mine) + partner[:, :64].astype(F32)
    stat = stat.astype(F32) + partner[:, 64:66].astype(F32)
    st_hi, st_lo = split_pair(jnp.sum(stat, axis=1, keepdims=True))
    packed_out = jnp.concatenate([normed_part.astype(BF), st_hi, st_lo, tail], axis=1)
    near = lax.ppermute(packed_out, "zlo", [(i, i ^ 1) for i in range(4)])
    far = lax.ppermute(packed_out, "zlo", [(i, i ^ 2) for i in range(4)])
    farther = lax.ppermute(packed_out, "zlo", [(i, i ^ 3) for i in range(4)])
    total = (packed_out.astype(F32) + near.astype(F32)) + (far.astype(F32) + farther.astype(F32))
    grad_normed = total[:, :64]
    row_stat = total[:, 64:65] + total[:, 65:66]
    normed = text_wide * inverse_rms
    grad_text = inverse_rms * (grad_normed * text_gain - normed * (row_stat / TEXT_DIM))
    return (grad_video, grad_text)


def solution(mesh):
    fine = Mesh(mesh.devices.reshape(4, 2, 4, 2, 4), ("x", "zhi", "y", "c", "zlo"))
    seq = ("x", "zhi", "y", "c")
    in_specs = (
        P(seq, None),
        P(seq, None),
        P(None, seq),
        P(seq),
        P(seq, "zlo"),
        P(seq, "zlo"),
        P(seq, "zlo"),
        P("zlo", seq),
    )
    out_specs = (P(seq, "zlo"), P(None, seq))
    return jax.shard_map(body, mesh=fine, in_specs=in_specs, out_specs=out_specs, check_vma=False)
```
